32 devices in a mesh: group: 2 (over y), wide: 4 (over z), sub: 2 (over x), pol: 2 (over core).
Axes of the slice: x: 2, y: 2, z: 4, core: 2. Of those that a mesh axis runs over, the one named last changes fastest.
Arguments:
- voltages: bfloat16 [2, 2048, 4, 2048], P('pol', ('group', 'wide'), 'sub'), parts along dimension 1, may hold values from -6 to 6
- real_weight: bfloat16 [512, 1024, 256], P(('wide', 'sub', 'pol')), may hold values from -0.125 to 0.125
- imaginary_weight: bfloat16 [512, 1024, 256], P(('wide', 'sub', 'pol')), may hold values from -0.125 to 0.125
- delays: int32 [128, 512], P('pol'), may hold values from 0 to 3
Outputs:
- dedispersed: float32 [512, 4, 128], P(('group', 'wide', 'sub'), None, 'pol'), parts along dimension 0
The draws below stay inside these ranges and needn't reach their ends.
There are 2 independent parts, one for each index of `group`. The reference program is written for one: setup_inputs(seed, part) draws one part's arguments, and reference() takes and returns one part's arrays. A program takes and returns all parts, laid end to end along the dimension named above; an argument that names none is the same for every part. Nothing has to cross between parts.
Inputs may be any that keep to these rules, and one draw needn't show every extreme that they name: `delays`: integer sample shifts of each delay trial and channel.
All inputs are finite; a program needn't handle non-finite values.
Results may differ from the reference program's by a relative error of at most 0.012.
Values may be sent and summed in bfloat16 or wider, within the bound.
A program may use at most 256 MiB of HBM per device.

```python
import math
import jax
import jax.numpy as jnp
from jax import lax

ANTENNA_COUNT = 1024
FRAME_SAMPLES = 2048
CHANNEL_COUNT = 512
BEAM_COUNT = 256
TRIALS = 128
FRAME_COUNT = 4


def plant(values, stream_key, least, largest):
    longest = values.shape.index(max(values.shape))
    spots = []
    for shift in (0, 1):
        where = [jax.random.randint(jax.random.fold_in(stream_key, axis), (), 0, length) for axis, length in enumerate(values.shape)]
        where[longest] = (where[longest] + shift) % values.shape[longest]
        spots.append(tuple(where))
    return values.at[spots[0]].set(least).at[spots[1]].set(largest)


def shard_levels(own_key, shape, split, low, largest):
    level = 1.0
    for dim, blocks in split:
        heights = jax.random.uniform(jax.random.fold_in(jax.random.fold_in(own_key, 6), dim), (blocks,), jnp.float32, low / len(split), largest / len(split))
        level = level * jnp.repeat(jnp.exp(heights), shape[dim] // blocks).reshape((-1,) + (1,) * (len(shape) - 1 - dim))
    return level


def normal_values(rng, dims, width, bound, split=(), dtype=jnp.bfloat16):
    values = width * jax.random.normal(rng, dims, jnp.float32)
    if split:
        values = values * shard_levels(rng, dims, split, -0.22, 0.18)
    return jnp.clip(values, -bound, bound).astype(dtype)


def setup_inputs(seed: int = 0, part: int = 0) -> dict:
    seeds = jax.random.split(jax.random.key(seed), 5)
    part_keys = jax.random.split(jax.random.fold_in(seeds[4], part), 5)
    return {
        "voltages": normal_values(part_keys[0], (2, ANTENNA_COUNT, FRAME_COUNT, FRAME_SAMPLES), 1.0, 6.0, ((0, 2), (1, 4), (2, 2))),
        "real_weight": normal_values(seeds[1], (CHANNEL_COUNT, ANTENNA_COUNT, BEAM_COUNT), (2 * ANTENNA_COUNT) ** -0.5, 0.125, ((0, 16),)),
        "imaginary_weight": normal_values(seeds[2], (CHANNEL_COUNT, ANTENNA_COUNT, BEAM_COUNT), (2 * ANTENNA_COUNT) ** -0.5, 0.125, ((0, 16),)),
        "delays": plant(jax.random.randint(seeds[3], (TRIALS, CHANNEL_COUNT), 0, FRAME_COUNT), jax.random.fold_in(seeds[3], 1), 0, FRAME_COUNT - 1).astype(jnp.int32),
    }


def reference(voltages, real_weight, imaginary_weight, delays):
    first_bin = FRAME_SAMPLES // 2 - CHANNEL_COUNT
    spectrum = jnp.fft.rfft(voltages.astype(jnp.float32), axis=-1)[..., first_bin:first_bin + CHANNEL_COUNT] / math.sqrt(FRAME_SAMPLES)
    x_re = jnp.real(spectrum).astype(jnp.bfloat16)
    x_im = jnp.imag(spectrum).astype(jnp.bfloat16)
    input_arrays = jnp.concatenate([x_re, x_im], axis=1)
    input_arrays = jnp.transpose(input_arrays, (3, 0, 2, 1)).reshape(CHANNEL_COUNT, 2 * FRAME_COUNT, 2 * ANTENNA_COUNT)
    channel_block = math.gcd(CHANNEL_COUNT, 16)

    def beam_tile(triple):
        left, real_part, imag_part = triple
        upper = jnp.concatenate([real_part, imag_part], axis=2)
        lower = jnp.concatenate([-imag_part, real_part], axis=2)
        real_form = jnp.concatenate([upper, lower], axis=1)
        return jnp.einsum('cra,cab->crb', left.astype(jnp.float32), real_form.astype(jnp.float32), precision=lax.Precision.HIGHEST)
    beam_output = lax.map(beam_tile, (input_arrays.reshape(-1, channel_block, 2 * FRAME_COUNT, 2 * ANTENNA_COUNT), real_weight.reshape(-1, channel_block, ANTENNA_COUNT, BEAM_COUNT), imaginary_weight.reshape(-1, channel_block, ANTENNA_COUNT, BEAM_COUNT)))
    beam_field = beam_output.reshape(CHANNEL_COUNT, 2, FRAME_COUNT, 2, BEAM_COUNT)
    power = lax.optimization_barrier(jnp.sum(beam_field * beam_field, axis=(1, 3)))
    centered = power - lax.optimization_barrier(jnp.mean(power, axis=1, keepdims=True))
    frame_ids = jnp.arange(FRAME_COUNT).astype(jnp.int32)

    def one_trial(delay_row):
        index = (frame_ids[None, :] + delay_row[:, None].astype(jnp.int32)) % FRAME_COUNT
        index = jnp.broadcast_to(index[:, :, None], centered.shape)
        return lax.optimization_barrier(jnp.sum(jnp.take_along_axis(centered, index, axis=1), axis=0))
    result = lax.map(one_trial, delays)
    return jnp.transpose(result, (2, 1, 0)) / math.sqrt(CHANNEL_COUNT)
```

```python
import functools
import math

import jax
import jax.numpy as jnp
import numpy as np
from jax import lax
from jax.experimental import pallas as pl
from jax.experimental.pallas import tpu as pltpu
from jax.sharding import PartitionSpec as P


def dft_table(sample_total, channel_total):
    first_bin = sample_total // 2 - channel_total
    freq_bins = first_bin + jnp.arange(channel_total, dtype=jnp.int32)
    sample_ids = jnp.arange(sample_total, dtype=jnp.int32)
    turns = freq_bins[:, None] * sample_ids[None, :] % sample_total
    angles = turns.astype(jnp.float32) * (2.0 * math.pi / sample_total)
    factor = 1.0 / math.sqrt(sample_total)
    exact = jnp.stack([jnp.cos(angles) * factor, -jnp.sin(angles) * factor], axis=1)
    upper = exact.astype(jnp.bfloat16)
    lower = (exact - upper.astype(jnp.float32)).astype(jnp.bfloat16)
    return jnp.stack([upper, lower], axis=2).reshape(4 * channel_total, sample_total)


def voltage_turn(blocks_in):
    result = lax.all_to_all(blocks_in, ("wide", "sub"), split_axis=0, concat_axis=0, tiled=True)
    return result


def pol_turn(blocks_in):
    return lax.all_to_all(blocks_in, "pol", split_axis=1, concat_axis=1, tiled=True)


def power_turn(blocks_in):
    result = lax.all_to_all(blocks_in, ("wide", "sub"), split_axis=0, concat_axis=0, tiled=True)
    return result


def dedisperse(power_all, delay_rows, frames, channel_total):
    frame_ids = jnp.arange(frames, dtype=jnp.int32)
    scale_step = 2.0 * math.pi / frames
    fwd_angle = (frame_ids[:, None] * frame_ids[None, :] % frames).astype(jnp.float32) * scale_step
    keeper = (frame_ids != 0).astype(jnp.float32)[:, None]
    fwd_cos = jnp.cos(fwd_angle) * keeper
    fwd_sin = jnp.sin(fwd_angle) * keeper
    spec_re = jnp.einsum("kn,cnb->kcb", fwd_cos, power_all, precision=lax.Precision.HIGHEST)
    spec_im = -jnp.einsum("kn,cnb->kcb", fwd_sin, power_all, precision=lax.Precision.HIGHEST)
    block = 8 if frames % 8 == 0 else frames
    beam_local = power_all.shape[2]
    trial_local = delay_rows.shape[0]

    def add_block(step_index, total):
        start = step_index * block
        freq_vals = start + jnp.arange(block, dtype=jnp.int32)
        turns = freq_vals[:, None, None] * delay_rows[None, :, :] % frames
        angles = turns.astype(jnp.float32) * scale_step
        rot_cos = jnp.cos(angles)
        rot_sin = jnp.sin(angles)
        part_re = lax.dynamic_slice_in_dim(spec_re, start, block, 0)
        part_im = lax.dynamic_slice_in_dim(spec_im, start, block, 0)
        sum_re = jnp.einsum(
            "ktc,kcb->ktb", rot_cos, part_re, precision=lax.Precision.HIGHEST
        ) - jnp.einsum("ktc,kcb->ktb", rot_sin, part_im, precision=lax.Precision.HIGHEST)
        sum_im = jnp.einsum(
            "ktc,kcb->ktb", rot_sin, part_re, precision=lax.Precision.HIGHEST
        ) + jnp.einsum("ktc,kcb->ktb", rot_cos, part_im, precision=lax.Precision.HIGHEST)
        back_angle = (freq_vals[:, None] * frame_ids[None, :] % frames).astype(
            jnp.float32
        ) * scale_step
        total = total + jnp.einsum(
            "ktb,kn->bnt", sum_re, jnp.cos(back_angle), precision=lax.Precision.HIGHEST
        )
        return total - jnp.einsum(
            "ktb,kn->bnt", sum_im, jnp.sin(back_angle), precision=lax.Precision.HIGHEST
        )

    initial = jnp.zeros((beam_local, frames, trial_local), jnp.float32)
    total = lax.fori_loop(0, frames // block, add_block, initial)
    return total * (1.0 / (frames * math.sqrt(channel_total)))


def staged_local(voltages, real_weight, imaginary_weight, delays):
    widening_count = lax.axis_size("wide")
    subband_count = lax.axis_size("sub")
    polar_count = lax.axis_size("pol")
    group_list = widening_count * subband_count
    antenna_slice = voltages.shape[1]
    frame_slice = voltages.shape[2]
    sample_total = voltages.shape[3]
    channel_pairs = real_weight.shape[0]
    beam_total = real_weight.shape[2]
    channel_total = channel_pairs * group_list * polar_count
    frames = subband_count * frame_slice
    sample_matrix = voltages[0].reshape(antenna_slice * frame_slice, sample_total)
    dft_weights = dft_table(sample_total, channel_total)
    weighted_product = lax.dot_general(
        dft_weights, sample_matrix, (((1,), (1,)), ((), ())), preferred_element_type=jnp.float32
    )
    spectrum_rows = (
        weighted_product.reshape(channel_total, 2, 2, antenna_slice * frame_slice)
        .sum(axis=2)
        .astype(jnp.bfloat16)
    )
    current_blocks = spectrum_rows.reshape(
        group_list, polar_count, channel_pairs * 2, antenna_slice * frame_slice
    )
    current_blocks = pol_turn(voltage_turn(current_blocks))
    voltage_collection = current_blocks.reshape(
        widening_count, subband_count, polar_count, channel_pairs, 2, antenna_slice, frame_slice
    )
    real_section = real_weight.reshape(channel_pairs, widening_count, antenna_slice, beam_total)
    imaginary_split = imaginary_weight.reshape(
        channel_pairs, widening_count, antenna_slice, beam_total
    )
    form_re = jnp.stack([real_section, -imaginary_split], axis=1)
    form_im = jnp.stack([imaginary_split, real_section], axis=1)
    real_form = jnp.stack([form_re, form_im], axis=4)
    beam_field = jnp.einsum(
        "wsqckaf,ckwaob->cqsfob", voltage_collection, real_form, preferred_element_type=jnp.float32
    )
    power_field = jnp.sum(beam_field * beam_field, axis=(1, 4)).reshape(
        channel_pairs, frames, beam_total
    )
    beam_local = beam_total // group_list
    outgoing = power_field.reshape(channel_pairs, frames, group_list, beam_local)
    outgoing = jnp.transpose(outgoing, (2, 0, 1, 3)).reshape(
        group_list, channel_pairs * frames * beam_local
    )
    arrived = power_turn(outgoing)
    both_pols = lax.all_gather(
        arrived.reshape(group_list, 1, channel_pairs * frames * beam_local),
        "pol",
        axis=1,
        tiled=True,
    )
    power_all = both_pols.reshape(channel_total, frames, beam_local)
    return dedisperse(power_all, delays, frames, channel_total)


MESH = pl.DeviceIdType.MESH


def flip(index, mask, size):
    out, bit = 0, 1
    while bit < size:
        own = (index // bit) % 2
        out = out + bit * ((1 - own) if (mask // bit) % 2 else own)
        bit *= 2
    return out


def window_kernel(
    dims, v_ref, wr_hbm, wi_hbm, d_ref, cb_ref, sb_ref, ca_ref, sa_ref, out_ref,
    wr, wi, table, sent, held, acc, power, outgoing, arrived, hot,
    w_sem, send_sem, recv_sem, own_sem, psend_sem, precv_sem,
):
    wides, subs, pols, fslice = dims
    per_wide = subs * pols
    owners = wides * per_wide
    antennas = v_ref.shape[1]
    samples = v_ref.shape[2]
    channels = wr.shape[0]
    beams = wr.shape[2]
    frames = subs * fslice
    trials, channel_total = d_ref.shape
    rows = 2 * channels
    beam_local = outgoing.shape[1]
    lanes = 128
    w, s, q = lax.axis_index("wide"), lax.axis_index("sub"), lax.axis_index("pol")

    def place(m):
        mw, ms, mq = m // per_wide, (m // pols) % subs, m % pols
        return flip(w, mw, wides), flip(s, ms, subs), flip(q, mq, pols)

    def ident(m):
        tw, ts, tq = place(m)
        return {"wide": tw, "sub": ts, "pol": tq}

    barrier = pltpu.get_barrier_semaphore()
    for m in range(1, owners):
        pl.semaphore_signal(barrier, inc=1, device_id=ident(m), device_id_type=MESH)

    loads = []
    for mw in range(wides):
        tw = flip(w, mw, wides)
        part = pl.ds(pl.multiple_of(tw * antennas, antennas), antennas)
        pair = []
        for k, (src, dst) in enumerate(((wr_hbm, wr), (wi_hbm, wi))):
            copy = pltpu.make_async_copy(src.at[:, part, :], dst.at[:, part, :], w_sem.at[mw, k])
            copy.start()
            pair.append(copy)
        loads.append(pair)

    chunk = per_wide * rows
    cycle = ca_ref.shape[1]
    copies = [None] * owners
    for j in range(wides):
        mw = wides - 1 - j
        tw = flip(w, mw, wides)
        base = pl.multiple_of(tw * chunk, chunk)

        def fill(n1, carry, base=base):
            cos_in = cb_ref[pl.ds(base, chunk), :].reshape(chunk // cycle, cycle, lanes)
            sin_in = sb_ref[pl.ds(base, chunk), :].reshape(chunk // cycle, cycle, lanes)
            value = cos_in * ca_ref[n1][None] - sin_in * sa_ref[n1][None]
            table[:, pl.ds(pl.multiple_of(n1 * lanes, lanes), lanes)] = value.reshape(chunk, lanes).astype(jnp.bfloat16)
            return carry

        lax.fori_loop(0, samples // lanes, fill, 0)
        for f in range(fslice):
            spectrum = lax.dot_general(
                table[...], v_ref[f], (((1,), (1,)), ((), ())), preferred_element_type=jnp.float32
            )
            sent[j, f] = spectrum.astype(jnp.bfloat16)
        if j == 0:
            pl.semaphore_wait(barrier, owners - 1)
        for r in reversed(range(per_wide)):
            m = mw * per_wide + r
            tw, ts, tq = place(m)
            part = pl.ds(pl.multiple_of((ts * pols + tq) * rows, rows), rows)
            source = sent.at[j, :, part, :]
            target = held.at[w, q * subs + s]
            if m == 0:
                copy = pltpu.make_async_copy(source, target, own_sem.at[0])
            else:
                copy = pltpu.make_async_remote_copy(
                    src_ref=source, dst_ref=target, send_sem=send_sem.at[m], recv_sem=recv_sem.at[m],
                    device_id=ident(m), device_id_type=MESH,
                )
            copy.start()
            copies[m] = copy

    per_tile = lanes // channels
    lane = lax.broadcasted_iota(jnp.int32, (lanes, lanes), 1)
    line = lax.broadcasted_iota(jnp.int32, (lanes, lanes), 0)
    frame_lane = lax.broadcasted_iota(jnp.int32, (trials, lanes), 1) // channels
    for i in range(per_tile):
        spread = (line == i * channels + lane % channels).astype(jnp.float32).astype(jnp.bfloat16)
        for t in range(channel_total // lanes):
            wrapped = (d_ref[:, t * lanes:(t + 1) * lanes] & (frames - 1)).astype(jnp.float32).astype(jnp.bfloat16)
            wide_delay = jnp.dot(wrapped, spread, preferred_element_type=jnp.float32)
            at = (t * per_tile + i) * lanes
            for n in range(frames):
                wanted = ((frame_lane - n) & (frames - 1)).astype(jnp.float32)
                hot[n * trials:(n + 1) * trials, at:at + lanes] = (wide_delay == wanted).astype(jnp.float32).astype(jnp.bfloat16)

    tile = 16
    group = tile // 2
    parts = per_wide * fslice
    member = lax.broadcasted_iota(jnp.int32, (parts * tile, antennas), 0) // 2 % group
    for mw in range(wides):
        tw = flip(w, mw, wides)
        for copy in loads[mw]:
            copy.wait()
        for r in range(per_wide):
            m = mw * per_wide + r
            if m == 0:
                copies[0].wait()
            else:
                copies[m].wait_recv()
        span = pl.ds(pl.multiple_of(tw * antennas, antennas), antennas)

        def beam(g, carry, tw=tw, span=span, mw=mw):
            left = held[tw, :, :, pl.ds(pl.multiple_of(g * tile, tile), tile), :].reshape(parts * tile, antennas)
            left = jnp.concatenate(
                [left * (member == c).astype(jnp.float32).astype(jnp.bfloat16) for c in range(group)], axis=1
            )
            for k, weight in enumerate((wr, wi)):
                right = weight[pl.ds(g * group, group), span, :].reshape(group * antennas, beams)
                product = jnp.dot(left, right, preferred_element_type=jnp.float32)
                for b in range(beams // lanes):
                    piece = product[:, b * lanes:(b + 1) * lanes]
                    at = k * (beams // lanes) + b
                    if mw == 0:
                        acc[g, at] = piece
                    else:
                        acc[g, at] = acc[g, at] + piece
            return carry

        lax.fori_loop(0, channels // group, beam, 0)

    for g in range(channels // group):
        half = parts * group
        for b in range(beams // lanes):
            re_re = acc[g, b, pl.ds(0, half, stride=2), :]
            im_re = acc[g, b, pl.ds(1, half, stride=2), :]
            re_im = acc[g, beams // lanes + b, pl.ds(0, half, stride=2), :]
            im_im = acc[g, beams // lanes + b, pl.ds(1, half, stride=2), :]
            y_re = re_re - im_im
            y_im = re_im + im_re
            both = (y_re * y_re + y_im * y_im).reshape(pols, frames, group, lanes)
            total = both[0]
            for k in range(1, pols):
                total = total + both[k]
            mean = total[0]
            for k in range(1, frames):
                mean = mean + total[k]
            centered = total - (mean * (1.0 / frames))[None]
            power[:, g * group:(g + 1) * group, b * lanes:(b + 1) * lanes] = centered

    turned = jnp.transpose(power[...].reshape(frames * channels, beams), (1, 0))
    outgoing[...] = turned.astype(jnp.bfloat16).reshape(outgoing.shape)
    mine = (w * subs + s) * pols + q
    slot = pl.ds(pl.multiple_of(mine * lanes, lanes), lanes)
    shares = []
    for m in reversed(range(owners)):
        tw, ts, tq = place(m)
        source = outgoing.at[tw * subs + ts]
        target = arrived.at[:, slot]
        if m == 0:
            copy = pltpu.make_async_copy(source, target, own_sem.at[1])
        else:
            copy = pltpu.make_async_remote_copy(
                src_ref=source, dst_ref=target, send_sem=psend_sem.at[m], recv_sem=precv_sem.at[m],
                device_id=ident(m), device_id_type=MESH,
            )
        copy.start()
        shares.append(copy)
    for m in range(1, owners):
        copies[m].wait_send()
    for copy in shares:
        copy.wait()
    result = lax.dot_general(
        arrived[...], hot[...], (((1,), (1,)), ((), ())), preferred_element_type=jnp.float32
    )
    out_ref[...] = result * (1.0 / math.sqrt(channel_total))


def twiddles(sample_total, channel_total):
    lanes = 128
    cycle = sample_total // lanes
    bins = sample_total // 2 - channel_total + np.arange(channel_total)
    step = 2.0 * math.pi / sample_total
    quarter = np.array([0.0, 0.5 * math.pi])
    inner = (bins[:, None] * np.arange(lanes)[None, :] % sample_total) * step
    inner = (inner[:, None, :] + quarter[None, :, None]).reshape(2 * channel_total, lanes)
    outer = (np.arange(cycle)[:, None] * lanes * bins[None, :cycle] % sample_total) * step
    outer = np.repeat(outer, 2, axis=1)[:, :, None] + np.zeros((1, 1, lanes))
    factor = 1.0 / math.sqrt(sample_total)
    return tuple(
        jnp.asarray(a.astype(np.float32))
        for a in (np.cos(inner) * factor, np.sin(inner) * factor, np.cos(outer), np.sin(outer))
    )


def window_local(voltages, real_weight, imaginary_weight, delays):
    wides, subs, pols = (lax.axis_size(a) for a in ("wide", "sub", "pol"))
    owners = wides * subs * pols
    _, antennas, fslice, samples = voltages.shape
    channels, antenna_total, beams = real_weight.shape
    trials, channel_total = delays.shape
    frames = subs * fslice
    beam_local = beams // (wides * subs)
    parts = subs * pols * fslice
    lanes = 128
    tables = twiddles(samples, channel_total)
    frame_major = jnp.transpose(voltages[0], (1, 0, 2))
    vmem = pl.BlockSpec(memory_space=pltpu.VMEM)
    anyspace = pl.BlockSpec(memory_space=pl.ANY)
    bf16, f32 = jnp.bfloat16, jnp.float32
    result = pl.pallas_call(
        functools.partial(window_kernel, (wides, subs, pols, fslice)),
        out_shape=jax.ShapeDtypeStruct((beam_local, frames * trials), f32),
        in_specs=[vmem, anyspace, anyspace, vmem, vmem, vmem, vmem, vmem],
        out_specs=vmem,
        scratch_shapes=[
            pltpu.VMEM(real_weight.shape, bf16),
            pltpu.VMEM(real_weight.shape, bf16),
            pltpu.VMEM((subs * pols * 2 * channels, samples), bf16),
            pltpu.VMEM((wides, fslice, subs * pols * 2 * channels, antennas), bf16),
            pltpu.VMEM((wides, subs * pols, fslice, 2 * channels, antennas), bf16),
            pltpu.VMEM((channels // 8, 2 * beams // lanes, parts * 16, lanes), f32),
            pltpu.VMEM((frames, channels, beams), f32),
            pltpu.VMEM((wides * subs, beam_local, lanes), bf16),
            pltpu.VMEM((beam_local, owners * lanes), bf16),
            pltpu.VMEM((frames * trials, owners * lanes), bf16),
            pltpu.SemaphoreType.DMA((wides, 2)),
            pltpu.SemaphoreType.DMA((owners,)),
            pltpu.SemaphoreType.DMA((owners,)),
            pltpu.SemaphoreType.DMA((2,)),
            pltpu.SemaphoreType.DMA((owners,)),
            pltpu.SemaphoreType.DMA((owners,)),
        ],
        compiler_params=pltpu.CompilerParams(
            collective_id=0, has_side_effects=True, vmem_limit_bytes=60 * 1024 * 1024
        ),
    )(frame_major, real_weight, imaginary_weight, delays, *tables)
    return result.reshape(beam_local, frames, trials)


def power_of_two(value):
    return value > 0 and value & (value - 1) == 0


def in_one_kernel(voltages, real_weight, delays):
    wides, subs, pols = (lax.axis_size(a) for a in ("wide", "sub", "pol"))
    _, antennas, fslice, samples = voltages.shape
    channels, _, beams = real_weight.shape
    frames = subs * fslice
    return (
        all(power_of_two(v) for v in (wides, subs, pols, frames))
        and channels % 8 == 0
        and frames * channels == 128
        and antennas % 128 == 0
        and beams % 128 == 0
        and beams % (wides * subs * 16) == 0
        and samples % 128 == 0
        and (subs * pols * channels) % (samples // 128) == 0
        and delays.shape[1] % 128 == 0
        and delays.shape[0] % 16 == 0
        and 4 * real_weight.size <= 36 * 1024 * 1024
    )


def local(voltages, real_weight, imaginary_weight, delays):
    if in_one_kernel(voltages, real_weight, delays):
        return window_local(voltages, real_weight, imaginary_weight, delays)
    return staged_local(voltages, real_weight, imaginary_weight, delays)


def solution(mesh):
    placed = (
        P("pol", ("group", "wide"), "sub", None),
        P(("wide", "sub", "pol"), None, None),
        P(("wide", "sub", "pol"), None, None),
        P("pol", None),
    )
    return jax.shard_map(
        local,
        mesh=mesh,
        in_specs=placed,
        out_specs=P(("group", "wide", "sub"), None, "pol"),
        check_vma=False,
    )
```

```python
import functools
import math

import jax
import jax.numpy as jnp
import numpy as np
from jax import lax
from jax.experimental import pallas as pl
from jax.experimental.pallas import tpu as pltpu
from jax.sharding import PartitionSpec as P


def dft_table(sample_total, channel_total):
    first_bin = sample_total // 2 - channel_total
    freq_bins = first_bin + jnp.arange(channel_total, dtype=jnp.int32)
    sample_ids = jnp.arange(sample_total, dtype=jnp.int32)
    turns = freq_bins[:, None] * sample_ids[None, :] % sample_total
    angles = turns.astype(jnp.float32) * (2.0 * math.pi / sample_total)
    factor = 1.0 / math.sqrt(sample_total)
    exact = jnp.stack([jnp.cos(angles) * factor, -jnp.sin(angles) * factor], axis=1)
    upper = exact.astype(jnp.bfloat16)
    lower = (exact - upper.astype(jnp.float32)).astype(jnp.bfloat16)
    return jnp.stack([upper, lower], axis=2).reshape(4 * channel_total, sample_total)


def voltage_turn(blocks_in):
    result = lax.all_to_all(blocks_in, ("wide", "sub"), split_axis=0, concat_axis=0, tiled=True)
    return result


def pol_turn(blocks_in):
    return lax.all_to_all(blocks_in, "pol", split_axis=1, concat_axis=1, tiled=True)


def power_turn(blocks_in):
    result = lax.all_to_all(blocks_in, ("wide", "sub"), split_axis=0, concat_axis=0, tiled=True)
    return result


def dedisperse(power_all, delay_rows, frames, channel_total):
    frame_ids = jnp.arange(frames, dtype=jnp.int32)
    scale_step = 2.0 * math.pi / frames
    fwd_angle = (frame_ids[:, None] * frame_ids[None, :] % frames).astype(jnp.float32) * scale_step
    keeper = (frame_ids != 0).astype(jnp.float32)[:, None]
    fwd_cos = jnp.cos(fwd_angle) * keeper
    fwd_sin = jnp.sin(fwd_angle) * keeper
    spec_re = jnp.einsum("kn,cnb->kcb", fwd_cos, power_all, precision=lax.Precision.HIGHEST)
    spec_im = -jnp.einsum("kn,cnb->kcb", fwd_sin, power_all, precision=lax.Precision.HIGHEST)
    block = 8 if frames % 8 == 0 else frames
    beam_local = power_all.shape[2]
    trial_local = delay_rows.shape[0]

    def add_block(step_index, total):
        start = step_index * block
        freq_vals = start + jnp.arange(block, dtype=jnp.int32)
        turns = freq_vals[:, None, None] * delay_rows[None, :, :] % frames
        angles = turns.astype(jnp.float32) * scale_step
        rot_cos = jnp.cos(angles)
        rot_sin = jnp.sin(angles)
        part_re = lax.dynamic_slice_in_dim(spec_re, start, block, 0)
        part_im = lax.dynamic_slice_in_dim(spec_im, start, block, 0)
        sum_re = jnp.einsum(
            "ktc,kcb->ktb", rot_cos, part_re, precision=lax.Precision.HIGHEST
        ) - jnp.einsum("ktc,kcb->ktb", rot_sin, part_im, precision=lax.Precision.HIGHEST)
        sum_im = jnp.einsum(
            "ktc,kcb->ktb", rot_sin, part_re, precision=lax.Precision.HIGHEST
        ) + jnp.einsum("ktc,kcb->ktb", rot_cos, part_im, precision=lax.Precision.HIGHEST)
        back_angle = (freq_vals[:, None] * frame_ids[None, :] % frames).astype(
            jnp.float32
        ) * scale_step
        total = total + jnp.einsum(
            "ktb,kn->bnt", sum_re, jnp.cos(back_angle), precision=lax.Precision.HIGHEST
        )
        return total - jnp.einsum(
            "ktb,kn->bnt", sum_im, jnp.sin(back_angle), precision=lax.Precision.HIGHEST
        )

    initial = jnp.zeros((beam_local, frames, trial_local), jnp.float32)
    total = lax.fori_loop(0, frames // block, add_block, initial)
    return total * (1.0 / (frames * math.sqrt(channel_total)))


def staged_local(voltages, real_weight, imaginary_weight, delays):
    widening_count = lax.axis_size("wide")
    subband_count = lax.axis_size("sub")
    polar_count = lax.axis_size("pol")
    group_list = widening_count * subband_count
    antenna_slice = voltages.shape[1]
    frame_slice = voltages.shape[2]
    sample_total = voltages.shape[3]
    channel_pairs = real_weight.shape[0]
    beam_total = real_weight.shape[2]
    channel_total = channel_pairs * group_list * polar_count
    frames = subband_count * frame_slice
    sample_matrix = voltages[0].reshape(antenna_slice * frame_slice, sample_total)
    dft_weights = dft_table(sample_total, channel_total)
    weighted_product = lax.dot_general(
        dft_weights, sample_matrix, (((1,), (1,)), ((), ())), preferred_element_type=jnp.float32
    )
    spectrum_rows = (
        weighted_product.reshape(channel_total, 2, 2, antenna_slice * frame_slice)
        .sum(axis=2)
        .astype(jnp.bfloat16)
    )
    current_blocks = spectrum_rows.reshape(
        group_list, polar_count, channel_pairs * 2, antenna_slice * frame_slice
    )
    current_blocks = pol_turn(voltage_turn(current_blocks))
    voltage_collection = current_blocks.reshape(
        widening_count, subband_count, polar_count, channel_pairs, 2, antenna_slice, frame_slice
    )
    real_section = real_weight.reshape(channel_pairs, widening_count, antenna_slice, beam_total)
    imaginary_split = imaginary_weight.reshape(
        channel_pairs, widening_count, antenna_slice, beam_total
    )
    form_re = jnp.stack([real_section, -imaginary_split], axis=1)
    form_im = jnp.stack([imaginary_split, real_section], axis=1)
    real_form = jnp.stack([form_re, form_im], axis=4)
    beam_field = jnp.einsum(
        "wsqckaf,ckwaob->cqsfob", voltage_collection, real_form, preferred_element_type=jnp.float32
    )
    power_field = jnp.sum(beam_field * beam_field, axis=(1, 4)).reshape(
        channel_pairs, frames, beam_total
    )
    beam_local = beam_total // group_list
    outgoing = power_field.reshape(channel_pairs, frames, group_list, beam_local)
    outgoing = jnp.transpose(outgoing, (2, 0, 1, 3)).reshape(
        group_list, channel_pairs * frames * beam_local
    )
    arrived = power_turn(outgoing)
    both_pols = lax.all_gather(
        arrived.reshape(group_list, 1, channel_pairs * frames * beam_local),
        "pol",
        axis=1,
        tiled=True,
    )
    power_all = both_pols.reshape(channel_total, frames, beam_local)
    return dedisperse(power_all, delays, frames, channel_total)


MESH = pl.DeviceIdType.MESH


def flip(index, mask, size):
    out, bit = 0, 1
    while bit < size:
        own = (index // bit) % 2
        out = out + bit * ((1 - own) if (mask // bit) % 2 else own)
        bit *= 2
    return out


def window_kernel(
    dims, v_ref, wr_hbm, wi_hbm, d_ref, cb_ref, sb_ref, ca_ref, sa_ref, out_ref,
    wr, wi, table, sent, held, acc, power, outgoing, arrived, hot,
    w_sem, send_sem, recv_sem, own_sem, psend_sem, precv_sem, fsend_sem, frecv_sem,
):
    wides, subs, pols, fslice = dims
    per_wide = subs * pols
    owners = wides * per_wide
    antennas = v_ref.shape[1]
    samples = v_ref.shape[2]
    channels = wr.shape[0]
    beams = wr.shape[2]
    frames = subs * fslice
    trials, channel_total = d_ref.shape
    rows = 2 * channels
    beam_local = outgoing.shape[1]
    lanes = 128
    w, s, q = lax.axis_index("wide"), lax.axis_index("sub"), lax.axis_index("pol")

    def place(m):
        mw, ms, mq = m // per_wide, (m // pols) % subs, m % pols
        return flip(w, mw, wides), flip(s, ms, subs), flip(q, mq, pols)

    def ident(m):
        tw, ts, tq = place(m)
        return {"wide": tw, "sub": ts, "pol": tq}

    barrier = pltpu.get_barrier_semaphore()
    for m in range(1, owners):
        pl.semaphore_signal(barrier, inc=1, device_id=ident(m), device_id_type=MESH)

    loads = []
    for mw in range(wides):
        tw = flip(w, mw, wides)
        part = pl.ds(pl.multiple_of(tw * antennas, antennas), antennas)
        pair = []
        for k, (src, dst) in enumerate(((wr_hbm, wr), (wi_hbm, wi))):
            copy = pltpu.make_async_copy(src.at[:, part, :], dst.at[:, part, :], w_sem.at[mw, k])
            copy.start()
            pair.append(copy)
        loads.append(pair)

    chunk = per_wide * rows
    cycle = ca_ref.shape[1]
    tile = 16
    group = tile // 2
    groups = channels // group
    last = wides // 2
    copies = [None] * owners
    fine = {}

    def spectra(base, count, j, start):
        def fill(n1, carry):
            cos_in = cb_ref[pl.ds(base, count), :].reshape(count // cycle, cycle, lanes)
            sin_in = sb_ref[pl.ds(base, count), :].reshape(count // cycle, cycle, lanes)
            value = cos_in * ca_ref[n1][None] - sin_in * sa_ref[n1][None]
            at = pl.ds(pl.multiple_of(n1 * lanes, lanes), lanes)
            table[:count, at] = value.reshape(count, lanes).astype(jnp.bfloat16)
            return carry

        lax.fori_loop(0, samples // lanes, fill, 0)
        for f in range(fslice):
            spectrum = lax.dot_general(
                table[:count, :], v_ref[f], (((1,), (1,)), ((), ())), preferred_element_type=jnp.float32
            )
            sent[j, f, start:start + count, :] = spectrum.astype(jnp.bfloat16)

    def ship(m, source, target, send, recv):
        if m == 0:
            copy = pltpu.make_async_copy(source, target, recv)
        else:
            copy = pltpu.make_async_remote_copy(
                src_ref=source, dst_ref=target, send_sem=send, recv_sem=recv,
                device_id=ident(m), device_id_type=MESH,
            )
        copy.start()
        return copy

    for j in range(wides):
        mw = wides - 1 - j
        tw = flip(w, mw, wides)
        if j == 0:
            half = pols * rows
            for h, ms in enumerate(reversed(range(subs))):
                ts = flip(s, ms, subs)
                spectra(pl.multiple_of((tw * subs + ts) * half, half), half, j, h * half)
                if h == 0:
                    pl.semaphore_wait(barrier, owners - 1)
                for mq in reversed(range(pols)):
                    m = mw * per_wide + ms * pols + mq
                    tq = flip(q, mq, pols)
                    part = pl.ds(pl.multiple_of(h * half + tq * rows, rows), rows)
                    copies[m] = ship(m, sent.at[j, :, part, :], held.at[w, q * subs + s], send_sem.at[m], recv_sem.at[m])
        else:
            spectra(pl.multiple_of(tw * chunk, chunk), chunk, j, 0)
            for g in range(groups if mw == last else 1):
                for r in reversed(range(per_wide)):
                    m = mw * per_wide + r
                    _, ts, tq = place(m)
                    if mw == last:
                        part = pl.ds(pl.multiple_of((ts * pols + tq) * rows + g * tile, tile), tile)
                        target = held.at[w, q * subs + s, :, g * tile:(g + 1) * tile, :]
                        fine[g, r] = ship(m, sent.at[j, :, part, :], target, fsend_sem.at[g, r], frecv_sem.at[g, r])
                    else:
                        part = pl.ds(pl.multiple_of((ts * pols + tq) * rows, rows), rows)
                        recv = own_sem.at[0] if m == 0 else recv_sem.at[m]
                        copies[m] = ship(m, sent.at[j, :, part, :], held.at[w, q * subs + s], send_sem.at[m], recv)

    per_tile = lanes // channels
    lane = lax.broadcasted_iota(jnp.int32, (lanes, lanes), 1)
    line = lax.broadcasted_iota(jnp.int32, (lanes, lanes), 0)
    frame_lane = lax.broadcasted_iota(jnp.int32, (trials, lanes), 1) // channels
    for i in range(per_tile):
        spread = (line == i * channels + lane % channels).astype(jnp.float32).astype(jnp.bfloat16)
        for t in range(channel_total // lanes):
            wrapped = (d_ref[:, t * lanes:(t + 1) * lanes] & (frames - 1)).astype(jnp.float32).astype(jnp.bfloat16)
            wide_delay = jnp.dot(wrapped, spread, preferred_element_type=jnp.float32)
            at = (t * per_tile + i) * lanes
            for n in range(frames):
                wanted = ((frame_lane - n) & (frames - 1)).astype(jnp.float32)
                hot[n * trials:(n + 1) * trials, at:at + lanes] = (wide_delay == wanted).astype(jnp.float32).astype(jnp.bfloat16)

    parts = per_wide * fslice
    member = lax.broadcasted_iota(jnp.int32, (parts * tile, antennas), 0) // 2 % group

    def beam(g, mw):
        tw = flip(w, mw, wides)
        span = pl.ds(pl.multiple_of(tw * antennas, antennas), antennas)
        left = held[tw, :, :, pl.ds(pl.multiple_of(g * tile, tile), tile), :].reshape(parts * tile, antennas)
        left = jnp.concatenate(
            [left * (member == c).astype(jnp.float32).astype(jnp.bfloat16) for c in range(group)], axis=1
        )
        for k, weight in enumerate((wr, wi)):
            right = weight[pl.ds(g * group, group), span, :].reshape(group * antennas, beams)
            product = jnp.dot(left, right, preferred_element_type=jnp.float32)
            for b in range(beams // lanes):
                piece = product[:, b * lanes:(b + 1) * lanes]
                at = k * (beams // lanes) + b
                if mw == 0:
                    acc[g, at] = piece
                else:
                    acc[g, at] = acc[g, at] + piece

    def strength(g):
        count = parts * group
        for b in range(beams // lanes):
            re_re = acc[g, b, pl.ds(0, count, stride=2), :]
            im_re = acc[g, b, pl.ds(1, count, stride=2), :]
            re_im = acc[g, beams // lanes + b, pl.ds(0, count, stride=2), :]
            im_im = acc[g, beams // lanes + b, pl.ds(1, count, stride=2), :]
            y_re = re_re - im_im
            y_im = re_im + im_re
            both = (y_re * y_re + y_im * y_im).reshape(pols, frames, group, lanes)
            total = both[0]
            for k in range(1, pols):
                total = total + both[k]
            mean = total[0]
            for k in range(1, frames):
                mean = mean + total[k]
            centered = total - (mean * (1.0 / frames))[None]
            power[:, g * group:(g + 1) * group, b * lanes:(b + 1) * lanes] = centered

    for mw in [0] + [k for k in reversed(range(1, wides)) if k != last]:
        for copy in loads[mw]:
            copy.wait()
        for r in range(per_wide):
            m = mw * per_wide + r
            if m == 0:
                copies[0].wait()
            else:
                copies[m].wait_recv()

        def whole(g, carry, mw=mw):
            beam(g, mw)
            return carry

        lax.fori_loop(0, groups, whole, 0)
    for copy in loads[last]:
        copy.wait()
    for g in range(groups):
        for r in range(per_wide):
            fine[g, r].wait_recv()
        beam(g, last)
        strength(g)

    turned = jnp.transpose(power[...].reshape(frames * channels, beams), (1, 0))
    outgoing[...] = turned.astype(jnp.bfloat16).reshape(outgoing.shape)
    mine = (w * subs + s) * pols + q
    slot = pl.ds(pl.multiple_of(mine * lanes, lanes), lanes)
    shares = []
    for m in reversed(range(owners)):
        tw, ts, tq = place(m)
        source = outgoing.at[tw * subs + ts]
        target = arrived.at[:, slot]
        if m == 0:
            copy = pltpu.make_async_copy(source, target, own_sem.at[1])
        else:
            copy = pltpu.make_async_remote_copy(
                src_ref=source, dst_ref=target, send_sem=psend_sem.at[m], recv_sem=precv_sem.at[m],
                device_id=ident(m), device_id_type=MESH,
            )
        copy.start()
        shares.append(copy)
    for copy in [c for c in copies[1:] if c is not None] + list(fine.values()):
        copy.wait_send()
    for copy in shares:
        copy.wait()
    result = lax.dot_general(
        arrived[...], hot[...], (((1,), (1,)), ((), ())), preferred_element_type=jnp.float32
    )
    result = result * (1.0 / math.sqrt(channel_total))
    for n in range(frames):
        out_ref[:, n, :] = result[:, n * trials:(n + 1) * trials]


def twiddles(sample_total, channel_total):
    lanes = 128
    cycle = sample_total // lanes
    bins = sample_total // 2 - channel_total + np.arange(channel_total)
    step = 2.0 * math.pi / sample_total
    quarter = np.array([0.0, 0.5 * math.pi])
    inner = (bins[:, None] * np.arange(lanes)[None, :] % sample_total) * step
    inner = (inner[:, None, :] + quarter[None, :, None]).reshape(2 * channel_total, lanes)
    outer = (np.arange(cycle)[:, None] * lanes * bins[None, :cycle] % sample_total) * step
    outer = np.repeat(outer, 2, axis=1)[:, :, None] + np.zeros((1, 1, lanes))
    factor = 1.0 / math.sqrt(sample_total)
    return tuple(
        jnp.asarray(a.astype(np.float32))
        for a in (np.cos(inner) * factor, np.sin(inner) * factor, np.cos(outer), np.sin(outer))
    )


def window_local(voltages, real_weight, imaginary_weight, delays):
    wides, subs, pols = (lax.axis_size(a) for a in ("wide", "sub", "pol"))
    owners = wides * subs * pols
    _, antennas, fslice, samples = voltages.shape
    channels, antenna_total, beams = real_weight.shape
    trials, channel_total = delays.shape
    frames = subs * fslice
    beam_local = beams // (wides * subs)
    parts = subs * pols * fslice
    lanes = 128
    tables = twiddles(samples, channel_total)
    frame_major = jnp.transpose(voltages[0], (1, 0, 2))
    vmem = pl.BlockSpec(memory_space=pltpu.VMEM)
    anyspace = pl.BlockSpec(memory_space=pl.ANY)
    bf16, f32 = jnp.bfloat16, jnp.float32
    result = pl.pallas_call(
        functools.partial(window_kernel, (wides, subs, pols, fslice)),
        out_shape=jax.ShapeDtypeStruct((beam_local, frames, trials), f32),
        in_specs=[vmem, anyspace, anyspace, vmem, vmem, vmem, vmem, vmem],
        out_specs=vmem,
        scratch_shapes=[
            pltpu.VMEM(real_weight.shape, bf16),
            pltpu.VMEM(real_weight.shape, bf16),
            pltpu.VMEM((subs * pols * 2 * channels, samples), bf16),
            pltpu.VMEM((wides, fslice, subs * pols * 2 * channels, antennas), bf16),
            pltpu.VMEM((wides, subs * pols, fslice, 2 * channels, antennas), bf16),
            pltpu.VMEM((channels // 8, 2 * beams // lanes, parts * 16, lanes), f32),
            pltpu.VMEM((frames, channels, beams), f32),
            pltpu.VMEM((wides * subs, beam_local, lanes), bf16),
            pltpu.VMEM((beam_local, owners * lanes), bf16),
            pltpu.VMEM((frames * trials, owners * lanes), bf16),
            pltpu.SemaphoreType.DMA((wides, 2)),
            pltpu.SemaphoreType.DMA((owners,)),
            pltpu.SemaphoreType.DMA((owners,)),
            pltpu.SemaphoreType.DMA((2,)),
            pltpu.SemaphoreType.DMA((owners,)),
            pltpu.SemaphoreType.DMA((owners,)),
            pltpu.SemaphoreType.DMA((channels // 8, subs * pols)),
            pltpu.SemaphoreType.DMA((channels // 8, subs * pols)),
        ],
        compiler_params=pltpu.CompilerParams(
            collective_id=0, has_side_effects=True, vmem_limit_bytes=60 * 1024 * 1024
        ),
    )(frame_major, real_weight, imaginary_weight, delays, *tables)
    return result


def power_of_two(value):
    return value > 0 and value & (value - 1) == 0


def in_one_kernel(voltages, real_weight, delays):
    wides, subs, pols = (lax.axis_size(a) for a in ("wide", "sub", "pol"))
    _, antennas, fslice, samples = voltages.shape
    channels, _, beams = real_weight.shape
    frames = subs * fslice
    return (
        all(power_of_two(v) for v in (wides, subs, pols, frames))
        and wides > 1
        and (pols * 2 * channels) % (samples // 128 * 2) == 0
        and channels % 8 == 0
        and frames * channels == 128
        and antennas % 128 == 0
        and beams % 128 == 0
        and beams % (wides * subs * 16) == 0
        and samples % 128 == 0
        and delays.shape[1] % 128 == 0
        and delays.shape[0] % 16 == 0
        and 4 * real_weight.size <= 36 * 1024 * 1024
    )


def local(voltages, real_weight, imaginary_weight, delays):
    if in_one_kernel(voltages, real_weight, delays):
        return window_local(voltages, real_weight, imaginary_weight, delays)
    return staged_local(voltages, real_weight, imaginary_weight, delays)


def solution(mesh):
    placed = (
        P("pol", ("group", "wide"), "sub", None),
        P(("wide", "sub", "pol"), None, None),
        P(("wide", "sub", "pol"), None, None),
        P("pol", None),
    )
    return jax.shard_map(
        local,
        mesh=mesh,
        in_specs=placed,
        out_specs=P(("group", "wide", "sub"), None, "pol"),
        check_vma=False,
    )
```

```python
import functools
import math

import jax
import jax.numpy as jnp
import numpy as np
from jax import lax
from jax.experimental import pallas as pl
from jax.experimental.pallas import tpu as pltpu
from jax.sharding import PartitionSpec as P


def dft_table(sample_total, channel_total):
    first_bin = sample_total // 2 - channel_total
    freq_bins = first_bin + jnp.arange(channel_total, dtype=jnp.int32)
    sample_ids = jnp.arange(sample_total, dtype=jnp.int32)
    turns = freq_bins[:, None] * sample_ids[None, :] % sample_total
    angles = turns.astype(jnp.float32) * (2.0 * math.pi / sample_total)
    factor = 1.0 / math.sqrt(sample_total)
    exact = jnp.stack([jnp.cos(angles) * factor, -jnp.sin(angles) * factor], axis=1)
    upper = exact.astype(jnp.bfloat16)
    lower = (exact - upper.astype(jnp.float32)).astype(jnp.bfloat16)
    return jnp.stack([upper, lower], axis=2).reshape(4 * channel_total, sample_total)


def voltage_turn(blocks_in):
    result = lax.all_to_all(blocks_in, ("wide", "sub"), split_axis=0, concat_axis=0, tiled=True)
    return result


def pol_turn(blocks_in):
    return lax.all_to_all(blocks_in, "pol", split_axis=1, concat_axis=1, tiled=True)


def power_turn(blocks_in):
    result = lax.all_to_all(blocks_in, ("wide", "sub"), split_axis=0, concat_axis=0, tiled=True)
    return result


def dedisperse(power_all, delay_rows, frames, channel_total):
    frame_ids = jnp.arange(frames, dtype=jnp.int32)
    scale_step = 2.0 * math.pi / frames
    fwd_angle = (frame_ids[:, None] * frame_ids[None, :] % frames).astype(jnp.float32) * scale_step
    keeper = (frame_ids != 0).astype(jnp.float32)[:, None]
    fwd_cos = jnp.cos(fwd_angle) * keeper
    fwd_sin = jnp.sin(fwd_angle) * keeper
    spec_re = jnp.einsum("kn,cnb->kcb", fwd_cos, power_all, precision=lax.Precision.HIGHEST)
    spec_im = -jnp.einsum("kn,cnb->kcb", fwd_sin, power_all, precision=lax.Precision.HIGHEST)
    block = 8 if frames % 8 == 0 else frames
    beam_local = power_all.shape[2]
    trial_local = delay_rows.shape[0]

    def add_block(step_index, total):
        start = step_index * block
        freq_vals = start + jnp.arange(block, dtype=jnp.int32)
        turns = freq_vals[:, None, None] * delay_rows[None, :, :] % frames
        angles = turns.astype(jnp.float32) * scale_step
        rot_cos = jnp.cos(angles)
        rot_sin = jnp.sin(angles)
        part_re = lax.dynamic_slice_in_dim(spec_re, start, block, 0)
        part_im = lax.dynamic_slice_in_dim(spec_im, start, block, 0)
        sum_re = jnp.einsum(
            "ktc,kcb->ktb", rot_cos, part_re, precision=lax.Precision.HIGHEST
        ) - jnp.einsum("ktc,kcb->ktb", rot_sin, part_im, precision=lax.Precision.HIGHEST)
        sum_im = jnp.einsum(
            "ktc,kcb->ktb", rot_sin, part_re, precision=lax.Precision.HIGHEST
        ) + jnp.einsum("ktc,kcb->ktb", rot_cos, part_im, precision=lax.Precision.HIGHEST)
        back_angle = (freq_vals[:, None] * frame_ids[None, :] % frames).astype(
            jnp.float32
        ) * scale_step
        total = total + jnp.einsum(
            "ktb,kn->bnt", sum_re, jnp.cos(back_angle), precision=lax.Precision.HIGHEST
        )
        return total - jnp.einsum(
            "ktb,kn->bnt", sum_im, jnp.sin(back_angle), precision=lax.Precision.HIGHEST
        )

    initial = jnp.zeros((beam_local, frames, trial_local), jnp.float32)
    total = lax.fori_loop(0, frames // block, add_block, initial)
    return total * (1.0 / (frames * math.sqrt(channel_total)))


def staged_local(voltages, real_weight, imaginary_weight, delays):
    widening_count = lax.axis_size("wide")
    subband_count = lax.axis_size("sub")
    polar_count = lax.axis_size("pol")
    group_list = widening_count * subband_count
    antenna_slice = voltages.shape[1]
    frame_slice = voltages.shape[2]
    sample_total = voltages.shape[3]
    channel_pairs = real_weight.shape[0]
    beam_total = real_weight.shape[2]
    channel_total = channel_pairs * group_list * polar_count
    frames = subband_count * frame_slice
    sample_matrix = voltages[0].reshape(antenna_slice * frame_slice, sample_total)
    dft_weights = dft_table(sample_total, channel_total)
    weighted_product = lax.dot_general(
        dft_weights, sample_matrix, (((1,), (1,)), ((), ())), preferred_element_type=jnp.float32
    )
    spectrum_rows = (
        weighted_product.reshape(channel_total, 2, 2, antenna_slice * frame_slice)
        .sum(axis=2)
        .astype(jnp.bfloat16)
    )
    current_blocks = spectrum_rows.reshape(
        group_list, polar_count, channel_pairs * 2, antenna_slice * frame_slice
    )
    current_blocks = pol_turn(voltage_turn(current_blocks))
    voltage_collection = current_blocks.reshape(
        widening_count, subband_count, polar_count, channel_pairs, 2, antenna_slice, frame_slice
    )
    real_section = real_weight.reshape(channel_pairs, widening_count, antenna_slice, beam_total)
    imaginary_split = imaginary_weight.reshape(
        channel_pairs, widening_count, antenna_slice, beam_total
    )
    form_re = jnp.stack([real_section, -imaginary_split], axis=1)
    form_im = jnp.stack([imaginary_split, real_section], axis=1)
    real_form = jnp.stack([form_re, form_im], axis=4)
    beam_field = jnp.einsum(
        "wsqckaf,ckwaob->cqsfob", voltage_collection, real_form, preferred_element_type=jnp.float32
    )
    power_field = jnp.sum(beam_field * beam_field, axis=(1, 4)).reshape(
        channel_pairs, frames, beam_total
    )
    beam_local = beam_total // group_list
    outgoing = power_field.reshape(channel_pairs, frames, group_list, beam_local)
    outgoing = jnp.transpose(outgoing, (2, 0, 1, 3)).reshape(
        group_list, channel_pairs * frames * beam_local
    )
    arrived = power_turn(outgoing)
    both_pols = lax.all_gather(
        arrived.reshape(group_list, 1, channel_pairs * frames * beam_local),
        "pol",
        axis=1,
        tiled=True,
    )
    power_all = both_pols.reshape(channel_total, frames, beam_local)
    return dedisperse(power_all, delays, frames, channel_total)


MESH = pl.DeviceIdType.MESH


def flip(index, mask, size):
    out, bit = 0, 1
    while bit < size:
        own = (index // bit) % 2
        out = out + bit * ((1 - own) if (mask // bit) % 2 else own)
        bit *= 2
    return out


def window_kernel(
    dims, raw_ref, wr_hbm, wi_hbm, d_ref, cb_ref, sb_ref, ca_ref, sa_ref, out_ref,
    wr, wi, v_ref, table, sent, held, acc, power, outgoing, arrived, hot,
    w_sem, send_sem, recv_sem, own_sem, psend_sem, precv_sem, fsend_sem, frecv_sem,
):
    wides, subs, pols, fslice = dims
    per_wide = subs * pols
    owners = wides * per_wide
    antennas = v_ref.shape[1]
    samples = v_ref.shape[2]
    channels = wr.shape[0]
    beams = wr.shape[2]
    frames = subs * fslice
    trials, channel_total = d_ref.shape
    rows = 2 * channels
    beam_local = outgoing.shape[1]
    lanes = 128
    w, s, q = lax.axis_index("wide"), lax.axis_index("sub"), lax.axis_index("pol")

    def place(m):
        mw, ms, mq = m // per_wide, (m // pols) % subs, m % pols
        return flip(w, mw, wides), flip(s, ms, subs), flip(q, mq, pols)

    def ident(m):
        tw, ts, tq = place(m)
        return {"wide": tw, "sub": ts, "pol": tq}

    barrier = pltpu.get_barrier_semaphore()
    for m in range(1, owners):
        pl.semaphore_signal(barrier, inc=1, device_id=ident(m), device_id_type=MESH)

    loads = []
    for mw in range(wides):
        tw = flip(w, mw, wides)
        part = pl.ds(pl.multiple_of(tw * antennas, antennas), antennas)
        pair = []
        for k, (src, dst) in enumerate(((wr_hbm, wr), (wi_hbm, wi))):
            copy = pltpu.make_async_copy(src.at[:, part, :], dst.at[:, part, :], w_sem.at[mw, k])
            copy.start()
            pair.append(copy)
        loads.append(pair)

    def part_frames(k, carry):
        at = pl.ds(pl.multiple_of(k * 16, 16), 16)
        for f in range(fslice):
            v_ref[f, at, :] = raw_ref[at, f, :]
        return carry

    lax.fori_loop(0, antennas // 16, part_frames, 0)
    chunk = per_wide * rows
    cycle = ca_ref.shape[1]
    tile = 16
    group = tile // 2
    groups = channels // group
    last = wides // 2
    copies = [None] * owners
    fine = {}

    def spectra(base, count, j, start):
        def fill(n1, carry):
            cos_in = cb_ref[pl.ds(base, count), :].reshape(count // cycle, cycle, lanes)
            sin_in = sb_ref[pl.ds(base, count), :].reshape(count // cycle, cycle, lanes)
            value = cos_in * ca_ref[n1][None] - sin_in * sa_ref[n1][None]
            at = pl.ds(pl.multiple_of(n1 * lanes, lanes), lanes)
            table[:count, at] = value.reshape(count, lanes).astype(jnp.bfloat16)
            return carry

        lax.fori_loop(0, samples // lanes, fill, 0)
        for f in range(fslice):
            spectrum = lax.dot_general(
                table[:count, :], v_ref[f], (((1,), (1,)), ((), ())), preferred_element_type=jnp.float32
            )
            sent[j, f, start:start + count, :] = spectrum.astype(jnp.bfloat16)

    def ship(m, source, target, send, recv):
        if m == 0:
            copy = pltpu.make_async_copy(source, target, recv)
        else:
            copy = pltpu.make_async_remote_copy(
                src_ref=source, dst_ref=target, send_sem=send, recv_sem=recv,
                device_id=ident(m), device_id_type=MESH,
            )
        copy.start()
        return copy

    for j in range(wides):
        mw = wides - 1 - j
        tw = flip(w, mw, wides)
        if j == 0:
            half = pols * rows
            for h, ms in enumerate(reversed(range(subs))):
                ts = flip(s, ms, subs)
                spectra(pl.multiple_of((tw * subs + ts) * half, half), half, j, h * half)
                if h == 0:
                    pl.semaphore_wait(barrier, owners - 1)
                for mq in reversed(range(pols)):
                    m = mw * per_wide + ms * pols + mq
                    tq = flip(q, mq, pols)
                    part = pl.ds(pl.multiple_of(h * half + tq * rows, rows), rows)
                    copies[m] = ship(m, sent.at[j, :, part, :], held.at[w, q * subs + s], send_sem.at[m], recv_sem.at[m])
        else:
            spectra(pl.multiple_of(tw * chunk, chunk), chunk, j, 0)
            for g in range(groups if mw == last else 1):
                for r in reversed(range(per_wide)):
                    m = mw * per_wide + r
                    _, ts, tq = place(m)
                    if mw == last:
                        part = pl.ds(pl.multiple_of((ts * pols + tq) * rows + g * tile, tile), tile)
                        target = held.at[w, q * subs + s, :, g * tile:(g + 1) * tile, :]
                        fine[g, r] = ship(m, sent.at[j, :, part, :], target, fsend_sem.at[g, r], frecv_sem.at[g, r])
                    else:
                        part = pl.ds(pl.multiple_of((ts * pols + tq) * rows, rows), rows)
                        recv = own_sem.at[0] if m == 0 else recv_sem.at[m]
                        copies[m] = ship(m, sent.at[j, :, part, :], held.at[w, q * subs + s], send_sem.at[m], recv)

    per_tile = lanes // channels
    lane = lax.broadcasted_iota(jnp.int32, (lanes, lanes), 1)
    line = lax.broadcasted_iota(jnp.int32, (lanes, lanes), 0)
    frame_lane = lax.broadcasted_iota(jnp.int32, (trials, lanes), 1) // channels
    for i in range(per_tile):
        spread = (line == i * channels + lane % channels).astype(jnp.float32).astype(jnp.bfloat16)
        for t in range(channel_total // lanes):
            wrapped = (d_ref[:, t * lanes:(t + 1) * lanes] & (frames - 1)).astype(jnp.float32).astype(jnp.bfloat16)
            wide_delay = jnp.dot(wrapped, spread, preferred_element_type=jnp.float32)
            at = (t * per_tile + i) * lanes
            for n in range(frames):
                wanted = ((frame_lane - n) & (frames - 1)).astype(jnp.float32)
                hot[n * trials:(n + 1) * trials, at:at + lanes] = (wide_delay == wanted).astype(jnp.float32).astype(jnp.bfloat16)

    parts = per_wide * fslice
    member = lax.broadcasted_iota(jnp.int32, (parts * tile, antennas), 0) // 2 % group

    def beam(g, mw):
        tw = flip(w, mw, wides)
        span = pl.ds(pl.multiple_of(tw * antennas, antennas), antennas)
        left = held[tw, :, :, pl.ds(pl.multiple_of(g * tile, tile), tile), :].reshape(parts * tile, antennas)
        left = jnp.concatenate(
            [left * (member == c).astype(jnp.float32).astype(jnp.bfloat16) for c in range(group)], axis=1
        )
        for k, weight in enumerate((wr, wi)):
            right = weight[pl.ds(g * group, group), span, :].reshape(group * antennas, beams)
            product = jnp.dot(left, right, preferred_element_type=jnp.float32)
            for b in range(beams // lanes):
                piece = product[:, b * lanes:(b + 1) * lanes]
                at = k * (beams // lanes) + b
                if mw == 0:
                    acc[g, at] = piece
                else:
                    acc[g, at] = acc[g, at] + piece

    def strength(g):
        count = parts * group
        for b in range(beams // lanes):
            re_re = acc[g, b, pl.ds(0, count, stride=2), :]
            im_re = acc[g, b, pl.ds(1, count, stride=2), :]
            re_im = acc[g, beams // lanes + b, pl.ds(0, count, stride=2), :]
            im_im = acc[g, beams // lanes + b, pl.ds(1, count, stride=2), :]
            y_re = re_re - im_im
            y_im = re_im + im_re
            both = (y_re * y_re + y_im * y_im).reshape(pols, frames, group, lanes)
            total = both[0]
            for k in range(1, pols):
                total = total + both[k]
            mean = total[0]
            for k in range(1, frames):
                mean = mean + total[k]
            centered = total - (mean * (1.0 / frames))[None]
            power[:, g * group:(g + 1) * group, b * lanes:(b + 1) * lanes] = centered

    for mw in [0] + [k for k in reversed(range(1, wides)) if k != last]:
        for copy in loads[mw]:
            copy.wait()
        for r in range(per_wide):
            m = mw * per_wide + r
            if m == 0:
                copies[0].wait()
            else:
                copies[m].wait_recv()

        def whole(g, carry, mw=mw):
            beam(g, mw)
            return carry

        lax.fori_loop(0, groups, whole, 0)
    for copy in loads[last]:
        copy.wait()
    for g in range(groups):
        for r in range(per_wide):
            fine[g, r].wait_recv()
        beam(g, last)
        strength(g)

    turned = jnp.transpose(power[...].reshape(frames * channels, beams), (1, 0))
    outgoing[...] = turned.astype(jnp.bfloat16).reshape(outgoing.shape)
    mine = (w * subs + s) * pols + q
    slot = pl.ds(pl.multiple_of(mine * lanes, lanes), lanes)
    shares = []
    for m in reversed(range(owners)):
        tw, ts, tq = place(m)
        source = outgoing.at[tw * subs + ts]
        target = arrived.at[:, slot]
        if m == 0:
            copy = pltpu.make_async_copy(source, target, own_sem.at[1])
        else:
            copy = pltpu.make_async_remote_copy(
                src_ref=source, dst_ref=target, send_sem=psend_sem.at[m], recv_sem=precv_sem.at[m],
                device_id=ident(m), device_id_type=MESH,
            )
        copy.start()
        shares.append(copy)
    for copy in [c for c in copies[1:] if c is not None] + list(fine.values()):
        copy.wait_send()
    for copy in shares:
        copy.wait()
    result = lax.dot_general(
        arrived[...], hot[...], (((1,), (1,)), ((), ())), preferred_element_type=jnp.float32
    )
    result = result * (1.0 / math.sqrt(channel_total))
    for n in range(frames):
        out_ref[:, n, :] = result[:, n * trials:(n + 1) * trials]


def twiddles(sample_total, channel_total):
    lanes = 128
    cycle = sample_total // lanes
    bins = sample_total // 2 - channel_total + np.arange(channel_total)
    step = 2.0 * math.pi / sample_total
    quarter = np.array([0.0, 0.5 * math.pi])
    inner = (bins[:, None] * np.arange(lanes)[None, :] % sample_total) * step
    inner = (inner[:, None, :] + quarter[None, :, None]).reshape(2 * channel_total, lanes)
    outer = (np.arange(cycle)[:, None] * lanes * bins[None, :cycle] % sample_total) * step
    outer = np.repeat(outer, 2, axis=1)[:, :, None] + np.zeros((1, 1, lanes))
    factor = 1.0 / math.sqrt(sample_total)
    return tuple(
        jnp.asarray(a.astype(np.float32))
        for a in (np.cos(inner) * factor, np.sin(inner) * factor, np.cos(outer), np.sin(outer))
    )


def window_local(voltages, real_weight, imaginary_weight, delays):
    wides, subs, pols = (lax.axis_size(a) for a in ("wide", "sub", "pol"))
    owners = wides * subs * pols
    _, antennas, fslice, samples = voltages.shape
    channels, antenna_total, beams = real_weight.shape
    trials, channel_total = delays.shape
    frames = subs * fslice
    beam_local = beams // (wides * subs)
    parts = subs * pols * fslice
    lanes = 128
    tables = twiddles(samples, channel_total)
    vmem = pl.BlockSpec(memory_space=pltpu.VMEM)
    anyspace = pl.BlockSpec(memory_space=pl.ANY)
    bf16, f32 = jnp.bfloat16, jnp.float32
    result = pl.pallas_call(
        functools.partial(window_kernel, (wides, subs, pols, fslice)),
        out_shape=jax.ShapeDtypeStruct((beam_local, frames, trials), f32),
        in_specs=[vmem, anyspace, anyspace, vmem, vmem, vmem, vmem, vmem],
        out_specs=vmem,
        scratch_shapes=[
            pltpu.VMEM(real_weight.shape, bf16),
            pltpu.VMEM(real_weight.shape, bf16),
            pltpu.VMEM((fslice, antennas, samples), bf16),
            pltpu.VMEM((subs * pols * 2 * channels, samples), bf16),
            pltpu.VMEM((wides, fslice, subs * pols * 2 * channels, antennas), bf16),
            pltpu.VMEM((wides, subs * pols, fslice, 2 * channels, antennas), bf16),
            pltpu.VMEM((channels // 8, 2 * beams // lanes, parts * 16, lanes), f32),
            pltpu.VMEM((frames, channels, beams), f32),
            pltpu.VMEM((wides * subs, beam_local, lanes), bf16),
            pltpu.VMEM((beam_local, owners * lanes), bf16),
            pltpu.VMEM((frames * trials, owners * lanes), bf16),
            pltpu.SemaphoreType.DMA((wides, 2)),
            pltpu.SemaphoreType.DMA((owners,)),
            pltpu.SemaphoreType.DMA((owners,)),
            pltpu.SemaphoreType.DMA((2,)),
            pltpu.SemaphoreType.DMA((owners,)),
            pltpu.SemaphoreType.DMA((owners,)),
            pltpu.SemaphoreType.DMA((channels // 8, subs * pols)),
            pltpu.SemaphoreType.DMA((channels // 8, subs * pols)),
        ],
        compiler_params=pltpu.CompilerParams(
            collective_id=0, has_side_effects=True, vmem_limit_bytes=60 * 1024 * 1024
        ),
    )(voltages[0], real_weight, imaginary_weight, delays, *tables)
    return result


def power_of_two(value):
    return value > 0 and value & (value - 1) == 0


def in_one_kernel(voltages, real_weight, delays):
    wides, subs, pols = (lax.axis_size(a) for a in ("wide", "sub", "pol"))
    _, antennas, fslice, samples = voltages.shape
    channels, _, beams = real_weight.shape
    frames = subs * fslice
    return (
        all(power_of_two(v) for v in (wides, subs, pols, frames))
        and wides > 1
        and (pols * 2 * channels) % (samples // 128 * 2) == 0
        and channels % 8 == 0
        and frames * channels == 128
        and antennas % 128 == 0
        and beams % 128 == 0
        and beams % (wides * subs * 16) == 0
        and samples % 128 == 0
        and delays.shape[1] % 128 == 0
        and delays.shape[0] % 16 == 0
        and 4 * real_weight.size <= 36 * 1024 * 1024
    )


def local(voltages, real_weight, imaginary_weight, delays):
    if in_one_kernel(voltages, real_weight, delays):
        return window_local(voltages, real_weight, imaginary_weight, delays)
    return staged_local(voltages, real_weight, imaginary_weight, delays)


def solution(mesh):
    placed = (
        P("pol", ("group", "wide"), "sub", None),
        P(("wide", "sub", "pol"), None, None),
        P(("wide", "sub", "pol"), None, None),
        P("pol", None),
    )
    return jax.shard_map(
        local,
        mesh=mesh,
        in_specs=placed,
        out_specs=P(("group", "wide", "sub"), None, "pol"),
        check_vma=False,
    )
```
